32 devices in a mesh: layer: 2 (over x), band: 16 (over z, y, core).
Axes of the slice: x: 2, y: 2, z: 4, core: 2. Of those that a mesh axis runs over, the one named last changes fastest.
Arguments:
- coeffs: bfloat16 [32, 128, 10240], P('layer', None, 'band'), may hold values from -6 to 6
- hamilton: bfloat16 [32, 7, 128, 128], P('layer'), may hold values from -0.1875 to 0.1875
- neighbors: int32 [32, 7], P('layer'), may hold values from -1 to 31, as said below
- basis: bfloat16 [32, 1728, 128], P(('layer', 'band')), may hold values from -0.5 to 0.5
- occupation: int32 [10240], replicated, may hold values from 0 to 3
Outputs:
- filtered: bfloat16 [32, 128, 10240], P('layer', None, 'band')
- density: float32 [32, 1728], P(('layer', 'band'))
The draws below stay inside these ranges and needn't reach their ends.
Inputs may be any that keep to these rules, and one draw needn't show every extreme that they name: `neighbors`: column 0 of row e is e itself; columns 1 to 4 are its neighbours along the two periodic in-plane directions, all in e's plane of 16 elements (rows e // 16 * 16 to that plus 16 - 1); columns 5 and 6 are the elements at the same lattice site in the previous and the next plane, -1 before the first and after the last plane. The numbering of sites within each plane is drawn.
All inputs are finite; a program needn't handle non-finite values.
Results may differ from the reference program's by a relative error of at most 0.0042.
Values may be sent and summed in bfloat16 or wider, within the bound.
A program may use at most 64 MiB of HBM per device.

```python
import jax
import jax.numpy as jnp
from jax import lax

NB = 128
NBAND = 10240
FY = 4
FZ = 4
ELEMS_DEV = 16
E = 32
GP = 1728
OWNERS = 32
N_BAND = 16


def draw_neighbors(key, part):
    face_size = FY * FZ
    planes = E // face_size
    plane_keys = jax.random.split(jax.random.fold_in(key, 17), planes)
    shuffled = jax.vmap(lambda subkey: jax.random.permutation(subkey, face_size))(plane_keys).astype(jnp.int32)
    element_at = jnp.arange(planes, dtype=jnp.int32)[:, None] * face_size + shuffled
    sites = jnp.arange(face_size, dtype=jnp.int32)
    site_y = sites // FZ
    site_z = sites % FZ
    y_minus = (site_y - 1) % FY * FZ + site_z
    y_plus = (site_y + 1) % FY * FZ + site_z
    z_minus = site_y * FZ + (site_z - 1) % FZ
    z_plus = site_y * FZ + (site_z + 1) % FZ
    missing = jnp.full((1, face_size), -1, jnp.int32)
    before = jnp.concatenate([missing, element_at[:-1]], axis=0)
    after = jnp.concatenate([element_at[1:], missing], axis=0)
    table = jnp.stack([element_at, element_at[:, y_minus], element_at[:, y_plus], element_at[:, z_minus], element_at[:, z_plus], before, after], axis=-1)
    result = jnp.zeros((E, 7), jnp.int32)
    return result.at[element_at.reshape(-1)].set(table.reshape(-1, 7))


def place_ends(array, key, smallest, top_value):
    index_at = [jax.random.randint(jax.random.fold_in(key, axis), (), 0, length) for axis, length in enumerate(array.shape)]
    main_axis = array.shape.index(max(array.shape))
    beside = index_at[:main_axis] + [(index_at[main_axis] + 1) % array.shape[main_axis]] + index_at[main_axis + 1:]
    return array.at[tuple(index_at)].set(smallest).at[tuple(beside)].set(top_value)


def steps_of(key, shape, cuts, low, top_value):
    loudness, own = 1.0, jax.random.fold_in(key, 6)
    for dim, blocks in cuts:
        heights = jnp.exp(jax.random.uniform(jax.random.fold_in(own, dim), (blocks,), jnp.float32, low / len(cuts), top_value / len(cuts)))
        loudness = loudness * jnp.repeat(heights, shape[dim] // blocks).reshape([-1 if axis == dim else 1 for axis in range(len(shape))])
    return loudness


def noise(key, shape, scale, most, pieces=(), kind=jnp.bfloat16):
    values = scale * jax.random.normal(key, shape, jnp.float32)
    if pieces:
        values = values * steps_of(key, shape, pieces, -0.22, 0.18)
    return jnp.clip(values, -most, most).astype(kind)


def setup_inputs(seed: int = 0) -> dict:
    seeds = jax.random.split(jax.random.key(seed), 6)
    coeffs = noise(seeds[0], (E, NB, NBAND), 1.0, 6.0, ((0, 2), (2, 16)))
    hamilton = noise(seeds[1], (E, 7, NB, NB), (7 * NB) ** -0.5, 0.1875, ((0, 2),))
    neighbors = draw_neighbors(jax.random.fold_in(seeds[5], 71), 0)
    basis = noise(seeds[3], (OWNERS, GP, NB), NB ** -0.5, 0.5, ((0, 32),))
    occupation = place_ends(jax.random.randint(seeds[4], (NBAND,), 0, 4), jax.random.fold_in(seeds[4], 1), 0, 3).astype(jnp.int32)
    return dict(coeffs=coeffs, hamilton=hamilton, neighbors=neighbors, basis=basis, occupation=occupation)


center = 0.5
half_width = 1.5


def apply_hamiltonian(source, hamilton, neighbors):
    usable = neighbors >= 0
    clipped = jnp.where(usable, neighbors, 0).astype(jnp.int32)

    def one_row(packed):
        blocks, lookup, allowed = packed
        nearby = source[lookup].astype(jnp.float32) * allowed.astype(jnp.float32)[:, None, None]
        return jnp.einsum("kij,kjb->ib", blocks.astype(jnp.float32), nearby)

    return lax.map(one_row, (hamilton, clipped, usable))


def reference(coeffs, hamilton, neighbors, basis, occupation):
    start_vals = coeffs.astype(jnp.float32)
    first_image = apply_hamiltonian(coeffs, hamilton, neighbors)
    filtered_once = ((first_image - center * start_vals) / half_width).astype(jnp.bfloat16)
    second_image = apply_hamiltonian(filtered_once, hamilton, neighbors)
    filtered = (2.0 * (second_image - center * filtered_once.astype(jnp.float32)) / half_width - start_vals).astype(jnp.bfloat16)
    weights = (1 + occupation).astype(jnp.float32) / (2.0 * NBAND)

    def owner_density(owner_id):
        layer_pos = owner_id // N_BAND
        band_pos = owner_id % N_BAND
        element = (layer_pos * ELEMS_DEV + band_pos % ELEMS_DEV).astype(jnp.int32)
        orbital = jnp.dot(basis[owner_id], filtered[element], preferred_element_type=jnp.float32)
        return jnp.sum(orbital * orbital * weights[None, :], axis=1)

    density = lax.map(owner_density, jnp.arange(OWNERS, dtype=jnp.int32))
    return filtered, density
```

```python
import functools

import jax
import jax.numpy as jnp
from jax import lax
from jax.experimental import pallas as pl
from jax.experimental.pallas import tpu as pltpu
from jax.sharding import PartitionSpec as P

FY = 4
FZ = 4
MESH = pl.DeviceIdType.MESH

center = 0.5
half_width = 1.5


def with_halo(array, sides, width):
    for axis, dim in sides:
        devices, length = (lax.axis_size(axis), array.shape[dim])
        up = [(i, (i + 1) % devices) for i in range(devices - 1)]
        down = [(j, i) for i, j in up]
        last = lax.slice_in_dim(array, length - width, length, axis=dim)
        first = lax.slice_in_dim(array, 0, width, axis=dim)
        before = lax.ppermute(last, axis, up)
        after = lax.ppermute(first, axis, down)
        array = jnp.concatenate([before, array, after], axis=dim)
    return array


def neighbor_product(blocks, nearby):
    return jnp.einsum("ekij,ekjb->eib", blocks, nearby, preferred_element_type=jnp.float32)


def general_body(coeffs, hamilton, neighbors, basis, occupation):
    elements = coeffs.shape[0]
    face_size = FY * FZ
    offset = lax.axis_index("layer") * elements - face_size
    usable = neighbors >= 0
    position = jnp.where(usable, neighbors - offset, 0)
    allowed = usable.astype(jnp.bfloat16)

    def operate(source):
        padded = with_halo(source, (("layer", 0),), face_size)
        inside = source[position[:, :5] - face_size]
        result = neighbor_product(hamilton[:, :5], inside)
        across = padded[position[:, 5:]] * allowed[:, 5:, None, None]
        return result + neighbor_product(hamilton[:, 5:], across)

    start_vals = coeffs.astype(jnp.float32)
    first_image = operate(coeffs)
    filtered_once = ((first_image - center * start_vals) / half_width).astype(jnp.bfloat16)
    second_image = operate(filtered_once)
    filtered = (
        2.0 * (second_image - center * filtered_once.astype(jnp.float32)) / half_width - start_vals
    ).astype(jnp.bfloat16)
    weights = (1 + occupation).astype(jnp.float32) / (2.0 * occupation.shape[0])
    copies = lax.axis_size("band") // elements
    duplicated = jnp.tile(filtered, (copies, 1, 1))
    regrouped = lax.all_to_all(duplicated, "band", split_axis=0, concat_axis=2, tiled=True)
    orbital = jnp.dot(basis[0], regrouped[0], preferred_element_type=jnp.float32)
    density = jnp.sum(orbital * orbital * weights[None, :], axis=1)[None, :]
    return (filtered, density)


def kernel(spans, nb, c_hbm, h_hbm, nbr_hbm, basis_hbm, occ_ref, filt_hbm, dens_ref, *scratch):
    count = len(spans)
    cown, cx, f1o, f1x, outv = (scratch[i * count:(i + 1) * count] for i in range(5))
    (hown, hx, basis_v, nx_v, nown, nx, gram, gsend, grecv,
     c_send, c_recv, hx_send, hx_recv, n_send, n_recv, f_send, f_recv, g_send, g_recv,
     lc_sem, lh_sem, lo_sem, misc_sem) = scratch[5 * count:]
    elements = c_hbm.shape[0]
    nbl = c_hbm.shape[2]
    layer, b = lax.axis_index("layer"), lax.axis_index("band")
    other = 1 - layer
    nz = nb // 4
    z, y, core = b // 4, (b // 2) % 2, b % 2
    own_cross, x_cross = 6 - layer, 6 - other

    def ident(zz, yy, cc):
        return zz * 4 + yy * 2 + cc

    n_copy = pltpu.make_async_copy(nbr_hbm, nown, misc_sem.at[0])
    n_copy.start()
    c_copies = []
    h_copies = [
        pltpu.make_async_copy(h_hbm.at[:, pl.ds(0, 5)], hown.at[:, pl.ds(0, 5)], lh_sem.at[0]),
        pltpu.make_async_copy(h_hbm.at[:, pl.ds(own_cross, 1)], hown.at[:, pl.ds(5, 1)], lh_sem.at[1]),
    ]

    barrier = pltpu.get_barrier_semaphore()
    pl.semaphore_signal(barrier, inc=1, device_id={"layer": other, "band": b}, device_id_type=MESH)
    for k in range(1, nb):
        pl.semaphore_signal(barrier, inc=1, device_id={"layer": layer, "band": (b + k) % nb}, device_id_type=MESH)
    pl.semaphore_wait(barrier, nb)

    def to_x(src, dst, send, recv):
        return pltpu.make_async_remote_copy(
            src_ref=src, dst_ref=dst, send_sem=send, recv_sem=recv,
            device_id={"layer": other, "band": b}, device_id_type=MESH)

    def to_band(src, dst, send, recv, peer):
        return pltpu.make_async_remote_copy(
            src_ref=src, dst_ref=dst, send_sem=send, recv_sem=recv,
            device_id={"layer": layer, "band": peer}, device_id_type=MESH)

    h_across = [
        to_x(h_hbm.at[b, pl.ds(0, 5)], hx.at[b, pl.ds(0, 5)], hx_send.at[0], hx_recv.at[0]),
        to_x(h_hbm.at[b, pl.ds(own_cross, 1)], hx.at[b, pl.ds(5, 1)], hx_send.at[1], hx_recv.at[1]),
    ]
    n_across = to_x(nbr_hbm, nx_v, n_send.at[0], n_recv.at[0])
    c_across = [
        to_x(c_hbm.at[:, :, pl.ds(lo, n)], cx[i], c_send.at[i], c_recv.at[i])
        for i, (lo, n) in enumerate(spans)
    ]
    for copy in h_across + [n_across] + c_across:
        copy.start()
    for i, (lo, n) in enumerate(spans):
        copy = pltpu.make_async_copy(c_hbm.at[:, :, pl.ds(lo, n)], cown[i], lc_sem.at[i])
        copy.start()
        c_copies.append(copy)
    for copy in h_copies:
        copy.start()
    b_copy = pltpu.make_async_copy(basis_hbm.at[0], basis_v, misc_sem.at[1])
    b_copy.start()

    sent = []

    def forward(block, peer):
        slot = len(sent)
        copy = to_band(hx.at[block], hx.at[block], f_send.at[slot], f_recv.at[block], peer)
        copy.start()
        sent.append(copy)

    def arrived(block, peer):
        to_band(hx.at[block], hx.at[block], f_send.at[0], f_recv.at[block], peer).wait_recv()

    y_peer, core_peer = ident(z, 1 - y, core), ident(z, y, 1 - core)
    for copy in h_across:
        copy.wait_recv()
    for k in range(1, nz):
        forward(b, ident((z + k) % nz, y, core))
    forward(b, y_peer)
    forward(b, core_peer)
    for k in range(1, nz):
        block = ident((z - k + nz) % nz, y, core)
        arrived(block, block)
        forward(block, y_peer)
        forward(block, core_peer)
    for k in range(nz):
        block = ident((z - k + nz) % nz, 1 - y, core)
        arrived(block, y_peer)
        forward(block, core_peer)
    for k in range(nz):
        for yy in (y, 1 - y):
            arrived(ident((z - k + nz) % nz, yy, 1 - core), core_peer)

    n_across.wait_recv()
    nx_copy = pltpu.make_async_copy(nx_v, nx, misc_sem.at[2])
    nx_copy.start()
    n_copy.wait()
    nx_copy.wait()
    for copy in h_copies:
        copy.wait()

    def image(blocks, table, e, cross, near, far):
        row = jnp.concatenate([blocks[e, k] for k in range(6)], axis=1)
        parts = [near[lax.rem(table[e, k], elements)] for k in range(5)]
        parts.append(far[lax.rem(table[e, cross], elements)])
        return jnp.dot(row, jnp.concatenate(parts, axis=0), preferred_element_type=jnp.float32)

    out_copies = []
    for i, (lo, n) in enumerate(spans):
        c_copies[i].wait()
        c_across[i].wait_recv()

        def first_own(e, carry):
            got = image(hown, nown, e, own_cross, cown[i], cx[i])
            f1o[i][e] = ((got - center * cown[i][e].astype(jnp.float32)) * (1.0 / half_width)).astype(jnp.bfloat16)
            return carry

        def first_x(e, carry):
            got = image(hx, nx, e, x_cross, cx[i], cown[i])
            f1x[i][e] = ((got - center * cx[i][e].astype(jnp.float32)) * (1.0 / half_width)).astype(jnp.bfloat16)
            return carry

        start = pl.multiple_of(b * nbl + lo, 128)
        weight = (1 + occ_ref[:, pl.ds(start, n)]).astype(jnp.float32)

        def second(e, carry):
            got = image(hown, nown, e, own_cross, f1o[i], f1x[i])
            once = f1o[i][e].astype(jnp.float32)
            value = (got - center * once) * (2.0 / half_width) - cown[i][e].astype(jnp.float32)
            value = value.astype(jnp.bfloat16)
            outv[i][e] = value
            scaled = (value.astype(jnp.float32) * weight).astype(jnp.bfloat16)
            part = lax.dot_general(scaled, value, (((1,), (1,)), ((), ())), preferred_element_type=jnp.float32)
            if i > 0:
                part = gram[e] + part
            if i == count - 1:
                gsend[e] = part.astype(jnp.bfloat16)
            gram[e] = part
            return carry

        lax.fori_loop(0, elements, first_own, 0)
        lax.fori_loop(0, elements, first_x, 0)
        lax.fori_loop(0, elements, second, 0)
        copy = pltpu.make_async_copy(outv[i], filt_hbm.at[:, :, pl.ds(lo, n)], lo_sem.at[i])
        copy.start()
        out_copies.append(copy)

    g_copies = []
    for k in range(1, nb):
        peer = (b + k) % nb
        copy = to_band(gsend.at[peer], grecv.at[k], g_send.at[k], g_recv.at[k], peer)
        copy.start()
        g_copies.append(copy)
    b_copy.wait()
    total = gram[b]
    for k in range(1, nb):
        g_copies[k - 1].wait_recv()
        total = total + grecv[k].astype(jnp.float32)
    total = total * (1.0 / (2.0 * nbl * nb))
    high = total.astype(jnp.bfloat16)
    low = (total - high.astype(jnp.float32)).astype(jnp.bfloat16)
    functions = basis_v[...]
    image_g = jnp.dot(functions, high, preferred_element_type=jnp.float32)
    image_g = image_g + jnp.dot(functions, low, preferred_element_type=jnp.float32)
    product = image_g * functions.astype(jnp.float32)
    top = product.astype(jnp.bfloat16)
    rest = (product - top.astype(jnp.float32)).astype(jnp.bfloat16)
    ones = jnp.ones((16, product.shape[1]), jnp.bfloat16)
    over_last = (((1,), (1,)), ((), ()))
    density = lax.dot_general(ones, top, over_last, preferred_element_type=jnp.float32)
    density = density + lax.dot_general(ones, rest, over_last, preferred_element_type=jnp.float32)
    dens_ref[...] = density[0:1]

    for copy in h_across + [n_across] + c_across + sent + g_copies:
        copy.wait_send()
    for copy in out_copies:
        copy.wait()


def plane_body(nb, coeffs, hamilton, neighbors, basis, occupation):
    elements, nbasis, nbl = coeffs.shape
    points = basis.shape[1]
    spans, lo = [], 0
    while lo < nbl:
        n = min(256, nbl - lo)
        spans.append((lo, n))
        lo += n
    count = len(spans)
    table = jnp.pad(neighbors, ((0, 0), (0, 128 - neighbors.shape[1])))
    values = [pltpu.VMEM((elements, nbasis, n), jnp.bfloat16) for _, n in spans]
    dma = pltpu.SemaphoreType.DMA
    hbm = pl.BlockSpec(memory_space=pl.ANY)
    vmem = pl.BlockSpec(memory_space=pltpu.VMEM)
    forwards = (nb // 4 - 1) + 2 + 2 * (nb // 4 - 1) + nb // 4
    return pl.pallas_call(
        functools.partial(kernel, spans, nb),
        out_shape=(
            jax.ShapeDtypeStruct(coeffs.shape, jnp.bfloat16),
            jax.ShapeDtypeStruct((1, points), jnp.float32),
        ),
        in_specs=[hbm, hbm, hbm, hbm, vmem],
        out_specs=(hbm, vmem),
        scratch_shapes=values * 5 + [
            pltpu.VMEM((elements, 6, nbasis, nbasis), jnp.bfloat16),
            pltpu.VMEM((elements, 6, nbasis, nbasis), jnp.bfloat16),
            pltpu.VMEM((points, nbasis), jnp.bfloat16),
            pltpu.VMEM((elements, 128), jnp.int32),
            pltpu.SMEM((elements, 128), jnp.int32),
            pltpu.SMEM((elements, 128), jnp.int32),
            pltpu.VMEM((elements, nbasis, nbasis), jnp.float32),
            pltpu.VMEM((elements, nbasis, nbasis), jnp.bfloat16),
            pltpu.VMEM((nb, nbasis, nbasis), jnp.bfloat16),
            dma((count,)), dma((count,)),
            dma((2,)), dma((2,)),
            dma((1,)), dma((1,)),
            dma((forwards,)), dma((nb,)),
            dma((nb,)), dma((nb,)),
            dma((count,)), dma((2,)), dma((count,)), dma((3,)),
        ],
        compiler_params=pltpu.CompilerParams(collective_id=0, has_side_effects=True),
    )(coeffs, hamilton, table, basis, occupation.reshape(1, -1))


def solution(mesh):
    layers, nb = mesh.shape["layer"], mesh.shape["band"]

    def body(coeffs, hamilton, neighbors, basis, occupation):
        elements = coeffs.shape[0]
        one_kernel = (
            layers == 2 and elements == FY * FZ and nb == elements
            and nb % 4 == 0 and coeffs.shape[2] % 128 == 0 and basis.shape[0] == 1
        )
        if one_kernel:
            return plane_body(nb, coeffs, hamilton, neighbors, basis, occupation)
        return general_body(coeffs, hamilton, neighbors, basis, occupation)

    return jax.shard_map(
        body,
        mesh=mesh,
        in_specs=(
            P("layer", None, "band"),
            P("layer", None, None, None),
            P("layer", None),
            P(("layer", "band"), None, None),
            P(),
        ),
        out_specs=(P("layer", None, "band"), P(("layer", "band"), None)),
        check_vma=False,
    )
```

```python
import functools

import jax
import jax.numpy as jnp
from jax import lax
from jax.experimental import pallas as pl
from jax.experimental.pallas import tpu as pltpu
from jax.sharding import PartitionSpec as P

FY = 4
FZ = 4
MESH = pl.DeviceIdType.MESH

center = 0.5
half_width = 1.5


def with_halo(array, sides, width):
    for axis, dim in sides:
        devices, length = (lax.axis_size(axis), array.shape[dim])
        up = [(i, (i + 1) % devices) for i in range(devices - 1)]
        down = [(j, i) for i, j in up]
        last = lax.slice_in_dim(array, length - width, length, axis=dim)
        first = lax.slice_in_dim(array, 0, width, axis=dim)
        before = lax.ppermute(last, axis, up)
        after = lax.ppermute(first, axis, down)
        array = jnp.concatenate([before, array, after], axis=dim)
    return array


def neighbor_product(blocks, nearby):
    return jnp.einsum("ekij,ekjb->eib", blocks, nearby, preferred_element_type=jnp.float32)


def general_body(coeffs, hamilton, neighbors, basis, occupation):
    elements = coeffs.shape[0]
    face_size = FY * FZ
    offset = lax.axis_index("layer") * elements - face_size
    usable = neighbors >= 0
    position = jnp.where(usable, neighbors - offset, 0)
    allowed = usable.astype(jnp.bfloat16)

    def operate(source):
        padded = with_halo(source, (("layer", 0),), face_size)
        inside = source[position[:, :5] - face_size]
        result = neighbor_product(hamilton[:, :5], inside)
        across = padded[position[:, 5:]] * allowed[:, 5:, None, None]
        return result + neighbor_product(hamilton[:, 5:], across)

    start_vals = coeffs.astype(jnp.float32)
    first_image = operate(coeffs)
    filtered_once = ((first_image - center * start_vals) / half_width).astype(jnp.bfloat16)
    second_image = operate(filtered_once)
    filtered = (
        2.0 * (second_image - center * filtered_once.astype(jnp.float32)) / half_width - start_vals
    ).astype(jnp.bfloat16)
    weights = (1 + occupation).astype(jnp.float32) / (2.0 * occupation.shape[0])
    copies = lax.axis_size("band") // elements
    duplicated = jnp.tile(filtered, (copies, 1, 1))
    regrouped = lax.all_to_all(duplicated, "band", split_axis=0, concat_axis=2, tiled=True)
    orbital = jnp.dot(basis[0], regrouped[0], preferred_element_type=jnp.float32)
    density = jnp.sum(orbital * orbital * weights[None, :], axis=1)[None, :]
    return (filtered, density)


def kernel(spans, nb, c_hbm, h_hbm, nbr_hbm, occ_ref, filt_hbm, total_ref, *scratch):
    count = len(spans)
    cown, cx, f1o, f1x, outv = (scratch[i * count:(i + 1) * count] for i in range(5))
    (hown, hx, nx_v, nown, nx, gram, gsend, gcore, grecv,
     c_send, c_recv, hx_send, hx_recv, n_send, n_recv, f_send, f_recv, k_send, k_recv, g_send, g_recv,
     lc_sem, lh_sem, lo_sem, misc_sem) = scratch[5 * count:]
    elements = c_hbm.shape[0]
    nbl = c_hbm.shape[2]
    layer, b = lax.axis_index("layer"), lax.axis_index("band")
    other = 1 - layer
    nz = nb // 4
    z, y, core = b // 4, (b // 2) % 2, b % 2
    own_cross, x_cross = 6 - layer, 6 - other

    def ident(zz, yy, cc):
        return zz * 4 + yy * 2 + cc

    n_copy = pltpu.make_async_copy(nbr_hbm, nown, misc_sem.at[0])
    n_copy.start()
    c_copies = []
    h_copies = [
        pltpu.make_async_copy(h_hbm.at[:, pl.ds(0, 5)], hown.at[:, pl.ds(0, 5)], lh_sem.at[0]),
        pltpu.make_async_copy(h_hbm.at[:, pl.ds(own_cross, 1)], hown.at[:, pl.ds(5, 1)], lh_sem.at[1]),
    ]

    barrier = pltpu.get_barrier_semaphore()
    pl.semaphore_signal(barrier, inc=1, device_id={"layer": other, "band": b}, device_id_type=MESH)
    half = nb // 2
    site = b // 2
    core_peer = b + 1 - 2 * core
    for peer in [core_peer] + [(site + k) % half * 2 + core for k in range(1, half)]:
        pl.semaphore_signal(barrier, inc=1, device_id={"layer": layer, "band": peer}, device_id_type=MESH)
    pl.semaphore_wait(barrier, half + 1)

    def to_x(src, dst, send, recv):
        return pltpu.make_async_remote_copy(
            src_ref=src, dst_ref=dst, send_sem=send, recv_sem=recv,
            device_id={"layer": other, "band": b}, device_id_type=MESH)

    def to_band(src, dst, send, recv, peer):
        return pltpu.make_async_remote_copy(
            src_ref=src, dst_ref=dst, send_sem=send, recv_sem=recv,
            device_id={"layer": layer, "band": peer}, device_id_type=MESH)

    h_across = [
        to_x(h_hbm.at[b, pl.ds(0, 5)], hx.at[b, pl.ds(0, 5)], hx_send.at[0], hx_recv.at[0]),
        to_x(h_hbm.at[b, pl.ds(own_cross, 1)], hx.at[b, pl.ds(5, 1)], hx_send.at[1], hx_recv.at[1]),
    ]
    n_across = to_x(nbr_hbm, nx_v, n_send.at[0], n_recv.at[0])
    c_across = [
        to_x(c_hbm.at[:, :, pl.ds(lo, n)], cx[i], c_send.at[i], c_recv.at[i])
        for i, (lo, n) in enumerate(spans)
    ]
    for copy in h_across + [n_across] + c_across:
        copy.start()
    for i, (lo, n) in enumerate(spans):
        copy = pltpu.make_async_copy(c_hbm.at[:, :, pl.ds(lo, n)], cown[i], lc_sem.at[i])
        copy.start()
        c_copies.append(copy)
    for copy in h_copies:
        copy.start()

    sent = []

    def forward(block, peer):
        slot = len(sent)
        copy = to_band(hx.at[block], hx.at[block], f_send.at[slot], f_recv.at[block], peer)
        copy.start()
        sent.append(copy)

    def arrived(block, peer):
        to_band(hx.at[block], hx.at[block], f_send.at[0], f_recv.at[block], peer).wait_recv()

    y_peer = ident(z, 1 - y, core)
    for copy in h_across:
        copy.wait_recv()
    for k in range(1, nz):
        forward(b, ident((z + k) % nz, y, core))
    forward(b, y_peer)
    forward(b, core_peer)
    for k in range(1, nz):
        block = ident((z - k + nz) % nz, y, core)
        arrived(block, block)
        forward(block, y_peer)
        forward(block, core_peer)
    for k in range(nz):
        block = ident((z - k + nz) % nz, 1 - y, core)
        arrived(block, y_peer)
        forward(block, core_peer)
    for k in range(nz):
        for yy in (y, 1 - y):
            arrived(ident((z - k + nz) % nz, yy, 1 - core), core_peer)

    n_across.wait_recv()
    nx_copy = pltpu.make_async_copy(nx_v, nx, misc_sem.at[1])
    nx_copy.start()
    n_copy.wait()
    nx_copy.wait()
    for copy in h_copies:
        copy.wait()

    def image(blocks, table, e, cross, near, far):
        row = jnp.concatenate([blocks[e, k] for k in range(6)], axis=1)
        parts = [near[lax.rem(table[e, k], elements)] for k in range(5)]
        parts.append(far[lax.rem(table[e, cross], elements)])
        return jnp.dot(row, jnp.concatenate(parts, axis=0), preferred_element_type=jnp.float32)

    out_copies = []
    for i, (lo, n) in enumerate(spans):
        c_copies[i].wait()
        c_across[i].wait_recv()

        last = i == count - 1
        start = pl.multiple_of(b * nbl + lo, 128)
        weight = (1 + occ_ref[:, pl.ds(start, n)]).astype(jnp.float32)

        def first_own(e):
            got = image(hown, nown, e, own_cross, cown[i], cx[i])
            return ((got - center * cown[i][e].astype(jnp.float32)) * (1.0 / half_width)).astype(jnp.bfloat16)

        def first_x(e):
            got = image(hx, nx, e, x_cross, cx[i], cown[i])
            return ((got - center * cx[i][e].astype(jnp.float32)) * (1.0 / half_width)).astype(jnp.bfloat16)

        step = 2 if last and elements % 2 == 0 else 1

        def first(t, carry):
            at = [t * step + u for u in range(step)]
            mine = [first_own(e) for e in at]
            theirs = [first_x(e) for e in at]
            for e, a, c in zip(at, mine, theirs):
                f1o[i][e] = a
                f1x[i][e] = c
            return carry

        def second(e):
            got = image(hown, nown, e, own_cross, f1o[i], f1x[i])
            once = f1o[i][e].astype(jnp.float32)
            value = (got - center * once) * (2.0 / half_width) - cown[i][e].astype(jnp.float32)
            value = value.astype(jnp.bfloat16)
            scaled = (value.astype(jnp.float32) * weight).astype(jnp.bfloat16)
            part = lax.dot_general(scaled, value, (((1,), (1,)), ((), ())), preferred_element_type=jnp.float32)
            return value, part + gram[e] if i > 0 else part

        def second_plain(e, carry):
            value, part = second(e)
            outv[i][e] = value
            gram[e] = part
            return carry

        def to_core(t):
            return to_band(gsend.at[2 * t + 1 - core], gcore.at[t], k_send.at[t], k_recv.at[t], core_peer)

        def to_owner(k):
            element = (site + k) % half * 2 + core
            return to_band(gsend.at[element], grecv.at[k], g_send.at[k], g_recv.at[k], element)

        def pair_up(s, carry):
            at = [2 * s, 2 * s + 1]
            got = [second(2 * t + 1 - core) for t in at]
            for t, (value, part) in zip(at, got):
                outv[i][2 * t + 1 - core] = value
                gsend[2 * t + 1 - core] = part.astype(jnp.bfloat16)
                to_core(t).start()
            return carry

        def hand_over(ks):
            places = [(site + k) % half for k in ks]
            got = [second(2 * t + core) for t in places]
            for k, t, (value, part) in zip(ks, places, got):
                outv[i][2 * t + core] = value
                to_core(t).wait_recv()
                part = part + gcore[t].astype(jnp.float32)
                if isinstance(k, int) and k == half:
                    gram[2 * t + core] = part
                else:
                    gsend[2 * t + core] = part.astype(jnp.bfloat16)
                    to_owner(k).start()

        def hand_over_two(s, carry):
            hand_over([2 * s + 1, 2 * s + 2])
            return carry

        lax.fori_loop(0, elements // step, first, 0)
        if last:
            lax.fori_loop(0, half // 2, pair_up, 0)
            lax.fori_loop(0, half // 2 - 1, hand_over_two, 0)
            hand_over([half - 1, half])
        else:
            lax.fori_loop(0, elements, second_plain, 0)
        copy = pltpu.make_async_copy(outv[i], filt_hbm.at[:, :, pl.ds(lo, n)], lo_sem.at[i])
        copy.start()
        out_copies.append(copy)

    total = gram[b]
    for k in range(1, half):
        to_owner(k).wait_recv()
        total = total + grecv[k].astype(jnp.float32)
    total_ref[...] = total * (1.0 / (2.0 * nbl * nb))

    for copy in h_across + [n_across] + c_across + sent:
        copy.wait_send()
    for t in range(half):
        to_core(t).wait_send()
    for k in range(1, half):
        to_owner(k).wait_send()
    for copy in out_copies:
        copy.wait()


def finish_kernel(pieces, filt_hbm, total_ref, basis_ref, out_hbm, dens_ref, held, in_sem, out_sem):
    size = held.shape[0] // pieces
    spans = [pl.ds(i * size, size) for i in range(pieces)]
    loads = [pltpu.make_async_copy(filt_hbm.at[at], held.at[at], in_sem.at[i]) for i, at in enumerate(spans)]
    stores = [pltpu.make_async_copy(held.at[at], out_hbm.at[at], out_sem.at[i]) for i, at in enumerate(spans)]
    for load in loads:
        load.start()
    for load, store in zip(loads, stores):
        load.wait()
        store.start()
    total = total_ref[...]
    high = total.astype(jnp.bfloat16)
    low = (total - high.astype(jnp.float32)).astype(jnp.bfloat16)
    functions = basis_ref[0]
    image_g = jnp.dot(functions, high, preferred_element_type=jnp.float32)
    image_g = image_g + jnp.dot(functions, low, preferred_element_type=jnp.float32)
    product = image_g * functions.astype(jnp.float32)
    top = product.astype(jnp.bfloat16)
    rest = (product - top.astype(jnp.float32)).astype(jnp.bfloat16)
    ones = jnp.ones((16, product.shape[1]), jnp.bfloat16)
    over_last = (((1,), (1,)), ((), ()))
    density = lax.dot_general(ones, top, over_last, preferred_element_type=jnp.float32)
    density = density + lax.dot_general(ones, rest, over_last, preferred_element_type=jnp.float32)
    dens_ref[...] = density[0:1]
    for store in stores:
        store.wait()


def plane_body(nb, coeffs, hamilton, neighbors, basis, occupation):
    elements, nbasis, nbl = coeffs.shape
    points = basis.shape[1]
    spans, lo = [], 0
    while lo < nbl:
        n = min(256, nbl - lo)
        spans.append((lo, n))
        lo += n
    count = len(spans)
    width = neighbors.shape[1]
    pieces = 4 if elements % 4 == 0 else 1
    values = [pltpu.VMEM((elements, nbasis, n), jnp.bfloat16) for _, n in spans]
    dma = pltpu.SemaphoreType.DMA
    hbm = pl.BlockSpec(memory_space=pl.ANY)
    vmem = pl.BlockSpec(memory_space=pltpu.VMEM)
    forwards = (nb // 4 - 1) + 2 + 2 * (nb // 4 - 1) + nb // 4
    spread, total = pl.pallas_call(
        functools.partial(kernel, spans, nb),
        out_shape=(
            jax.ShapeDtypeStruct(coeffs.shape, jnp.bfloat16),
            jax.ShapeDtypeStruct((nbasis, nbasis), jnp.float32),
        ),
        in_specs=[hbm, hbm, hbm, vmem],
        out_specs=(hbm, vmem),
        scratch_shapes=values * 5 + [
            pltpu.VMEM((elements, 6, nbasis, nbasis), jnp.bfloat16),
            pltpu.VMEM((elements, 6, nbasis, nbasis), jnp.bfloat16),
            pltpu.VMEM((elements, width), jnp.int32),
            pltpu.SMEM((elements, width), jnp.int32),
            pltpu.SMEM((elements, width), jnp.int32),
            pltpu.VMEM((elements, nbasis, nbasis), jnp.float32),
            pltpu.VMEM((elements, nbasis, nbasis), jnp.bfloat16),
            pltpu.VMEM((nb // 2, nbasis, nbasis), jnp.bfloat16),
            pltpu.VMEM((nb // 2, nbasis, nbasis), jnp.bfloat16),
            dma((count,)), dma((count,)),
            dma((2,)), dma((2,)),
            dma((1,)), dma((1,)),
            dma((forwards,)), dma((nb,)),
            dma((nb // 2,)), dma((nb // 2,)),
            dma((nb // 2,)), dma((nb // 2,)),
            dma((count,)), dma((2,)), dma((count,)), dma((2,)),
        ],
        compiler_params=pltpu.CompilerParams(collective_id=0, has_side_effects=True),
    )(coeffs, hamilton, neighbors, occupation.reshape(1, -1))
    return pl.pallas_call(
        functools.partial(finish_kernel, pieces),
        out_shape=(
            jax.ShapeDtypeStruct(coeffs.shape, jnp.bfloat16),
            jax.ShapeDtypeStruct((1, points), jnp.float32),
        ),
        in_specs=[hbm, vmem, vmem],
        out_specs=(hbm, vmem),
        scratch_shapes=[pltpu.VMEM(coeffs.shape, jnp.bfloat16), dma((pieces,)), dma((pieces,))],
    )(spread, total, basis)


def solution(mesh):
    layers, nb = mesh.shape["layer"], mesh.shape["band"]

    def body(coeffs, hamilton, neighbors, basis, occupation):
        elements = coeffs.shape[0]
        one_kernel = (
            layers == 2 and elements == FY * FZ and nb == elements
            and nb % 4 == 0 and nb >= 8 and coeffs.shape[2] % 128 == 0 and basis.shape[0] == 1
        )
        if one_kernel:
            return plane_body(nb, coeffs, hamilton, neighbors, basis, occupation)
        return general_body(coeffs, hamilton, neighbors, basis, occupation)

    return jax.shard_map(
        body,
        mesh=mesh,
        in_specs=(
            P("layer", None, "band"),
            P("layer", None, None, None),
            P("layer", None),
            P(("layer", "band"), None, None),
            P(),
        ),
        out_specs=(P("layer", None, "band"), P(("layer", "band"), None)),
        check_vma=False,
    )
```

```python
import functools

import jax
import jax.numpy as jnp
from jax import lax
from jax.experimental import pallas as pl
from jax.experimental.pallas import tpu as pltpu
from jax.sharding import PartitionSpec as P

FY = 4
FZ = 4
MESH = pl.DeviceIdType.MESH

center = 0.5
half_width = 1.5


def with_halo(array, sides, width):
    for axis, dim in sides:
        devices, length = (lax.axis_size(axis), array.shape[dim])
        up = [(i, (i + 1) % devices) for i in range(devices - 1)]
        down = [(j, i) for i, j in up]
        last = lax.slice_in_dim(array, length - width, length, axis=dim)
        first = lax.slice_in_dim(array, 0, width, axis=dim)
        before = lax.ppermute(last, axis, up)
        after = lax.ppermute(first, axis, down)
        array = jnp.concatenate([before, array, after], axis=dim)
    return array


def neighbor_product(blocks, nearby):
    return jnp.einsum("ekij,ekjb->eib", blocks, nearby, preferred_element_type=jnp.float32)


def general_body(coeffs, hamilton, neighbors, basis, occupation):
    elements = coeffs.shape[0]
    face_size = FY * FZ
    offset = lax.axis_index("layer") * elements - face_size
    usable = neighbors >= 0
    position = jnp.where(usable, neighbors - offset, 0)
    allowed = usable.astype(jnp.bfloat16)

    def operate(source):
        padded = with_halo(source, (("layer", 0),), face_size)
        inside = source[position[:, :5] - face_size]
        result = neighbor_product(hamilton[:, :5], inside)
        across = padded[position[:, 5:]] * allowed[:, 5:, None, None]
        return result + neighbor_product(hamilton[:, 5:], across)

    start_vals = coeffs.astype(jnp.float32)
    first_image = operate(coeffs)
    filtered_once = ((first_image - center * start_vals) / half_width).astype(jnp.bfloat16)
    second_image = operate(filtered_once)
    filtered = (
        2.0 * (second_image - center * filtered_once.astype(jnp.float32)) / half_width - start_vals
    ).astype(jnp.bfloat16)
    weights = (1 + occupation).astype(jnp.float32) / (2.0 * occupation.shape[0])
    copies = lax.axis_size("band") // elements
    duplicated = jnp.tile(filtered, (copies, 1, 1))
    regrouped = lax.all_to_all(duplicated, "band", split_axis=0, concat_axis=2, tiled=True)
    orbital = jnp.dot(basis[0], regrouped[0], preferred_element_type=jnp.float32)
    density = jnp.sum(orbital * orbital * weights[None, :], axis=1)[None, :]
    return (filtered, density)


def kernel(spans, nb, c_hbm, h_hbm, nbr_hbm, occ_ref, filt_hbm, total_ref, *scratch):
    count = len(spans)
    cown, cx, f1o, f1x, outv = (scratch[i * count:(i + 1) * count] for i in range(5))
    (hown, hx, nx_v, nown, nx, early, gram, gsend, gcore, grecv,
     c_send, c_recv, hx_send, hx_recv, n_send, n_recv, f_send, f_recv, k_send, k_recv, g_send, g_recv,
     lc_sem, lh_sem, lo_sem, misc_sem) = scratch[5 * count:]
    elements = c_hbm.shape[0]
    nbl = c_hbm.shape[2]
    layer, b = lax.axis_index("layer"), lax.axis_index("band")
    other = 1 - layer
    nz = nb // 4
    z, y, core = b // 4, (b // 2) % 2, b % 2
    own_cross, x_cross = 6 - layer, 6 - other

    def ident(zz, yy, cc):
        return zz * 4 + yy * 2 + cc

    n_copy = pltpu.make_async_copy(nbr_hbm, nown, misc_sem.at[0])
    n_copy.start()
    c_copies = []
    h_copies = [
        pltpu.make_async_copy(h_hbm.at[:, pl.ds(0, 5)], hown.at[:, pl.ds(0, 5)], lh_sem.at[0]),
        pltpu.make_async_copy(h_hbm.at[:, pl.ds(own_cross, 1)], hown.at[:, pl.ds(5, 1)], lh_sem.at[1]),
    ]

    barrier = pltpu.get_barrier_semaphore()
    pl.semaphore_signal(barrier, inc=1, device_id={"layer": other, "band": b}, device_id_type=MESH)
    half = nb // 2
    site = b // 2
    core_peer = b + 1 - 2 * core
    for peer in [core_peer] + [(site + k) % half * 2 + core for k in range(1, half)]:
        pl.semaphore_signal(barrier, inc=1, device_id={"layer": layer, "band": peer}, device_id_type=MESH)
    pl.semaphore_wait(barrier, half + 1)

    def to_x(src, dst, send, recv):
        return pltpu.make_async_remote_copy(
            src_ref=src, dst_ref=dst, send_sem=send, recv_sem=recv,
            device_id={"layer": other, "band": b}, device_id_type=MESH)

    def to_band(src, dst, send, recv, peer):
        return pltpu.make_async_remote_copy(
            src_ref=src, dst_ref=dst, send_sem=send, recv_sem=recv,
            device_id={"layer": layer, "band": peer}, device_id_type=MESH)

    h_across = [
        to_x(h_hbm.at[b, pl.ds(0, 5)], hx.at[b, pl.ds(0, 5)], hx_send.at[0], hx_recv.at[0]),
        to_x(h_hbm.at[b, pl.ds(own_cross, 1)], hx.at[b, pl.ds(5, 1)], hx_send.at[1], hx_recv.at[1]),
    ]
    n_across = to_x(nbr_hbm, nx_v, n_send.at[0], n_recv.at[0])
    c_across = [
        to_x(c_hbm.at[:, :, pl.ds(lo, n)], cx[i], c_send.at[i], c_recv.at[i])
        for i, (lo, n) in enumerate(spans)
    ]
    for copy in h_across + [n_across] + c_across:
        copy.start()
    for i, (lo, n) in enumerate(spans):
        copy = pltpu.make_async_copy(c_hbm.at[:, :, pl.ds(lo, n)], cown[i], lc_sem.at[i])
        copy.start()
        c_copies.append(copy)
    for copy in h_copies:
        copy.start()

    sent = []

    def forward(block, peer):
        slot = len(sent)
        copy = to_band(hx.at[block], hx.at[block], f_send.at[slot], f_recv.at[block], peer)
        copy.start()
        sent.append(copy)

    def arrived(block, peer):
        to_band(hx.at[block], hx.at[block], f_send.at[0], f_recv.at[block], peer).wait_recv()

    y_peer = ident(z, 1 - y, core)
    for copy in h_across:
        copy.wait_recv()
    for k in range(1, nz):
        forward(b, ident((z + k) % nz, y, core))
    forward(b, y_peer)
    forward(b, core_peer)
    for k in range(1, nz):
        block = ident((z - k + nz) % nz, y, core)
        arrived(block, block)
        forward(block, y_peer)
        forward(block, core_peer)
    for k in range(nz):
        block = ident((z - k + nz) % nz, 1 - y, core)
        arrived(block, y_peer)
        forward(block, core_peer)
    for k in range(nz):
        for yy in (y, 1 - y):
            arrived(ident((z - k + nz) % nz, yy, 1 - core), core_peer)

    n_across.wait_recv()
    nx_copy = pltpu.make_async_copy(nx_v, nx, misc_sem.at[1])
    nx_copy.start()
    n_copy.wait()
    nx_copy.wait()
    for copy in h_copies:
        copy.wait()

    def image(blocks, table, e, cross, near, far):
        row = jnp.concatenate([blocks[e, k] for k in range(6)], axis=1)
        parts = [near[lax.rem(table[k, e], elements)] for k in range(5)]
        parts.append(far[lax.rem(table[cross, e], elements)])
        return jnp.dot(row, jnp.concatenate(parts, axis=0), preferred_element_type=jnp.float32)

    out_copies = []
    for i, (lo, n) in enumerate(spans):
        c_copies[i].wait()
        last = i == count - 1

        def inside(e, carry):
            row = jnp.concatenate([hown[e, k] for k in range(5)], axis=1)
            parts = [cown[i][lax.rem(nown[k, e], elements)] for k in range(5)]
            got = jnp.dot(row, jnp.concatenate(parts, axis=0), preferred_element_type=jnp.float32)
            early[e] = got - center * cown[i][e].astype(jnp.float32)
            return carry

        if last:
            lax.fori_loop(0, elements, inside, 0)
        c_across[i].wait_recv()

        start = pl.multiple_of(b * nbl + lo, 128)
        weight = (1 + occ_ref[:, pl.ds(start, n)]).astype(jnp.float32)

        def first_own(e):
            if last:
                across = cx[i][lax.rem(nown[own_cross, e], elements)]
                got = early[e] + jnp.dot(hown[e, 5], across, preferred_element_type=jnp.float32)
                return (got * (1.0 / half_width)).astype(jnp.bfloat16)
            got = image(hown, nown, e, own_cross, cown[i], cx[i])
            return ((got - center * cown[i][e].astype(jnp.float32)) * (1.0 / half_width)).astype(jnp.bfloat16)

        def first_x(e):
            got = image(hx, nx, e, x_cross, cx[i], cown[i])
            return ((got - center * cx[i][e].astype(jnp.float32)) * (1.0 / half_width)).astype(jnp.bfloat16)

        step = 2 if last and elements % 2 == 0 else 1

        def first(t, carry):
            at = [t * step + u for u in range(step)]
            mine = [first_own(e) for e in at]
            theirs = [first_x(e) for e in at]
            for e, a, c in zip(at, mine, theirs):
                f1o[i][e] = a
                f1x[i][e] = c
            return carry

        def second(e):
            got = image(hown, nown, e, own_cross, f1o[i], f1x[i])
            once = f1o[i][e].astype(jnp.float32)
            value = (got - center * once) * (2.0 / half_width) - cown[i][e].astype(jnp.float32)
            value = value.astype(jnp.bfloat16)
            scaled = (value.astype(jnp.float32) * weight).astype(jnp.bfloat16)
            part = lax.dot_general(scaled, value, (((1,), (1,)), ((), ())), preferred_element_type=jnp.float32)
            return value, part + gram[e] if i > 0 else part

        def second_plain(e, carry):
            value, part = second(e)
            outv[i][e] = value
            gram[e] = part
            return carry

        def to_core(t):
            return to_band(gsend.at[2 * t + 1 - core], gcore.at[t], k_send.at[t], k_recv.at[t], core_peer)

        def to_owner(k):
            element = (site + k) % half * 2 + core
            return to_band(gsend.at[element], grecv.at[k], g_send.at[k], g_recv.at[k], element)

        def pair_up(s, carry):
            at = [2 * s, 2 * s + 1]
            got = [second(2 * t + 1 - core) for t in at]
            for t, (value, part) in zip(at, got):
                outv[i][2 * t + 1 - core] = value
                gsend[2 * t + 1 - core] = part.astype(jnp.bfloat16)
                to_core(t).start()
            return carry

        def hand_over(ks):
            places = [(site + k) % half for k in ks]
            got = [second(2 * t + core) for t in places]
            for k, t, (value, part) in zip(ks, places, got):
                outv[i][2 * t + core] = value
                to_core(t).wait_recv()
                part = part + gcore[t].astype(jnp.float32)
                if isinstance(k, int) and k == half:
                    gram[2 * t + core] = part
                else:
                    gsend[2 * t + core] = part.astype(jnp.bfloat16)
                    to_owner(k).start()

        def hand_over_two(s, carry):
            hand_over([half // 2 + s, half // 2 - s - 1])
            return carry

        lax.fori_loop(0, elements // step, first, 0)
        if last:
            lax.fori_loop(0, half // 2, pair_up, 0)
            lax.fori_loop(0, half // 2 - 1, hand_over_two, 0)
            hand_over([half - 1, half])
        else:
            lax.fori_loop(0, elements, second_plain, 0)
        copy = pltpu.make_async_copy(outv[i], filt_hbm.at[:, :, pl.ds(lo, n)], lo_sem.at[i])
        copy.start()
        out_copies.append(copy)

    total = gram[b]
    for k in range(1, half):
        to_owner(k).wait_recv()
        total = total + grecv[k].astype(jnp.float32)
    total_ref[...] = total * (1.0 / (2.0 * nbl * nb))

    for copy in h_across + [n_across] + c_across + sent:
        copy.wait_send()
    for t in range(half):
        to_core(t).wait_send()
    for k in range(1, half):
        to_owner(k).wait_send()
    for copy in out_copies:
        copy.wait()


def finish_kernel(pieces, filt_hbm, total_ref, basis_hbm, out_hbm, dens_ref, held, basis_v, in_sem, out_sem, basis_sem):
    size = held.shape[0] // pieces
    spans = [pl.ds(i * size, size) for i in range(pieces)]
    loads = [pltpu.make_async_copy(filt_hbm.at[at], held.at[at], in_sem.at[i]) for i, at in enumerate(spans)]
    stores = [pltpu.make_async_copy(held.at[at], out_hbm.at[at], out_sem.at[i]) for i, at in enumerate(spans)]
    basis_copy = pltpu.make_async_copy(basis_hbm.at[0], basis_v, basis_sem.at[0])
    loads[0].start()
    basis_copy.start()
    for load in loads[1:]:
        load.start()
    for load, store in zip(loads, stores):
        load.wait()
        store.start()
    total = total_ref[...]
    high = total.astype(jnp.bfloat16)
    low = (total - high.astype(jnp.float32)).astype(jnp.bfloat16)
    basis_copy.wait()
    functions = basis_v[...]
    image_g = jnp.dot(functions, high, preferred_element_type=jnp.float32)
    image_g = image_g + jnp.dot(functions, low, preferred_element_type=jnp.float32)
    product = image_g * functions.astype(jnp.float32)
    top = product.astype(jnp.bfloat16)
    rest = (product - top.astype(jnp.float32)).astype(jnp.bfloat16)
    ones = jnp.ones((16, product.shape[1]), jnp.bfloat16)
    over_last = (((1,), (1,)), ((), ()))
    density = lax.dot_general(ones, top, over_last, preferred_element_type=jnp.float32)
    density = density + lax.dot_general(ones, rest, over_last, preferred_element_type=jnp.float32)
    dens_ref[...] = density[0:1]
    for store in stores:
        store.wait()


def plane_body(nb, coeffs, hamilton, neighbors, basis, occupation):
    elements, nbasis, nbl = coeffs.shape
    points = basis.shape[1]
    spans, lo = [], 0
    while lo < nbl:
        n = min(256, nbl - lo)
        spans.append((lo, n))
        lo += n
    count = len(spans)
    width = neighbors.shape[1]
    pieces = 8 if elements % 8 == 0 else 1
    values = [pltpu.VMEM((elements, nbasis, n), jnp.bfloat16) for _, n in spans]
    dma = pltpu.SemaphoreType.DMA
    hbm = pl.BlockSpec(memory_space=pl.ANY)
    vmem = pl.BlockSpec(memory_space=pltpu.VMEM)
    forwards = (nb // 4 - 1) + 2 + 2 * (nb // 4 - 1) + nb // 4
    spread, total = pl.pallas_call(
        functools.partial(kernel, spans, nb),
        out_shape=(
            jax.ShapeDtypeStruct(coeffs.shape, jnp.bfloat16),
            jax.ShapeDtypeStruct((nbasis, nbasis), jnp.float32),
        ),
        in_specs=[hbm, hbm, hbm, vmem],
        out_specs=(hbm, vmem),
        scratch_shapes=values * 5 + [
            pltpu.VMEM((elements, 6, nbasis, nbasis), jnp.bfloat16),
            pltpu.VMEM((elements, 6, nbasis, nbasis), jnp.bfloat16),
            pltpu.VMEM((width, elements), jnp.int32),
            pltpu.SMEM((width, elements), jnp.int32),
            pltpu.SMEM((width, elements), jnp.int32),
            pltpu.VMEM((elements, nbasis, spans[-1][1]), jnp.float32),
            pltpu.VMEM((elements, nbasis, nbasis), jnp.float32),
            pltpu.VMEM((elements, nbasis, nbasis), jnp.bfloat16),
            pltpu.VMEM((nb // 2, nbasis, nbasis), jnp.bfloat16),
            pltpu.VMEM((nb // 2, nbasis, nbasis), jnp.bfloat16),
            dma((count,)), dma((count,)),
            dma((2,)), dma((2,)),
            dma((1,)), dma((1,)),
            dma((forwards,)), dma((nb,)),
            dma((nb // 2,)), dma((nb // 2,)),
            dma((nb // 2,)), dma((nb // 2,)),
            dma((count,)), dma((2,)), dma((count,)), dma((2,)),
        ],
        compiler_params=pltpu.CompilerParams(collective_id=0, has_side_effects=True),
    )(coeffs, hamilton, neighbors.T, occupation.reshape(1, -1))
    return pl.pallas_call(
        functools.partial(finish_kernel, pieces),
        out_shape=(
            jax.ShapeDtypeStruct(coeffs.shape, jnp.bfloat16),
            jax.ShapeDtypeStruct((1, points), jnp.float32),
        ),
        in_specs=[hbm, vmem, hbm],
        out_specs=(hbm, vmem),
        scratch_shapes=[
            pltpu.VMEM(coeffs.shape, jnp.bfloat16),
            pltpu.VMEM((points, nbasis), jnp.bfloat16),
            dma((pieces,)), dma((pieces,)), dma((1,)),
        ],
    )(spread, total, basis)


def solution(mesh):
    layers, nb = mesh.shape["layer"], mesh.shape["band"]

    def body(coeffs, hamilton, neighbors, basis, occupation):
        elements = coeffs.shape[0]
        one_kernel = (
            layers == 2 and elements == FY * FZ and nb == elements
            and nb % 4 == 0 and nb >= 8 and coeffs.shape[2] % 128 == 0 and basis.shape[0] == 1
        )
        if one_kernel:
            return plane_body(nb, coeffs, hamilton, neighbors, basis, occupation)
        return general_body(coeffs, hamilton, neighbors, basis, occupation)

    return jax.shard_map(
        body,
        mesh=mesh,
        in_specs=(
            P("layer", None, "band"),
            P("layer", None, None, None),
            P("layer", None),
            P(("layer", "band"), None, None),
            P(),
        ),
        out_specs=(P("layer", None, "band"), P(("layer", "band"), None)),
        check_vma=False,
    )
```

```python
import functools

import jax
import jax.numpy as jnp
from jax import lax
from jax.experimental import pallas as pl
from jax.experimental.pallas import tpu as pltpu
from jax.sharding import PartitionSpec as P

FY = 4
FZ = 4
MESH = pl.DeviceIdType.MESH

center = 0.5
half_width = 1.5


def with_halo(array, sides, width):
    for axis, dim in sides:
        devices, length = (lax.axis_size(axis), array.shape[dim])
        up = [(i, (i + 1) % devices) for i in range(devices - 1)]
        down = [(j, i) for i, j in up]
        last = lax.slice_in_dim(array, length - width, length, axis=dim)
        first = lax.slice_in_dim(array, 0, width, axis=dim)
        before = lax.ppermute(last, axis, up)
        after = lax.ppermute(first, axis, down)
        array = jnp.concatenate([before, array, after], axis=dim)
    return array


def neighbor_product(blocks, nearby):
    return jnp.einsum("ekij,ekjb->eib", blocks, nearby, preferred_element_type=jnp.float32)


def general_body(coeffs, hamilton, neighbors, basis, occupation):
    elements = coeffs.shape[0]
    face_size = FY * FZ
    offset = lax.axis_index("layer") * elements - face_size
    usable = neighbors >= 0
    position = jnp.where(usable, neighbors - offset, 0)
    allowed = usable.astype(jnp.bfloat16)

    def operate(source):
        padded = with_halo(source, (("layer", 0),), face_size)
        inside = source[position[:, :5] - face_size]
        result = neighbor_product(hamilton[:, :5], inside)
        across = padded[position[:, 5:]] * allowed[:, 5:, None, None]
        return result + neighbor_product(hamilton[:, 5:], across)

    start_vals = coeffs.astype(jnp.float32)
    first_image = operate(coeffs)
    filtered_once = ((first_image - center * start_vals) / half_width).astype(jnp.bfloat16)
    second_image = operate(filtered_once)
    filtered = (
        2.0 * (second_image - center * filtered_once.astype(jnp.float32)) / half_width - start_vals
    ).astype(jnp.bfloat16)
    weights = (1 + occupation).astype(jnp.float32) / (2.0 * occupation.shape[0])
    copies = lax.axis_size("band") // elements
    duplicated = jnp.tile(filtered, (copies, 1, 1))
    regrouped = lax.all_to_all(duplicated, "band", split_axis=0, concat_axis=2, tiled=True)
    orbital = jnp.dot(basis[0], regrouped[0], preferred_element_type=jnp.float32)
    density = jnp.sum(orbital * orbital * weights[None, :], axis=1)[None, :]
    return (filtered, density)


def kernel(spans, nb, c_hbm, h_hbm, nbr_hbm, occ_ref, filt_hbm, total_ref, *scratch):
    count = len(spans)
    cown, cx, f1o, f1x, outv = (scratch[i * count:(i + 1) * count] for i in range(5))
    (hown, hx, nx_v, nown, nx, gram, gsend, gcore, grecv,
     c_send, c_recv, hx_send, hx_recv, n_send, n_recv, f_send, f_recv, k_send, k_recv, g_send, g_recv,
     lc_sem, lh_sem, lo_sem, misc_sem) = scratch[5 * count:]
    elements = c_hbm.shape[0]
    nbl = c_hbm.shape[2]
    layer, b = lax.axis_index("layer"), lax.axis_index("band")
    other = 1 - layer
    nz = nb // 4
    z, y, core = b // 4, (b // 2) % 2, b % 2
    own_cross, x_cross = 6 - layer, 6 - other

    def ident(zz, yy, cc):
        return zz * 4 + yy * 2 + cc

    n_copy = pltpu.make_async_copy(nbr_hbm, nown, misc_sem.at[0])
    n_copy.start()
    c_copies = []
    h_copies = [
        pltpu.make_async_copy(h_hbm.at[:, pl.ds(0, 5)], hown.at[:, pl.ds(0, 5)], lh_sem.at[0]),
        pltpu.make_async_copy(h_hbm.at[:, pl.ds(own_cross, 1)], hown.at[:, pl.ds(5, 1)], lh_sem.at[1]),
    ]

    barrier = pltpu.get_barrier_semaphore()
    pl.semaphore_signal(barrier, inc=1, device_id={"layer": other, "band": b}, device_id_type=MESH)
    half = nb // 2
    site = b // 2
    core_peer = b + 1 - 2 * core
    for peer in [core_peer] + [(site + k) % half * 2 + core for k in range(1, half)]:
        pl.semaphore_signal(barrier, inc=1, device_id={"layer": layer, "band": peer}, device_id_type=MESH)
    pl.semaphore_wait(barrier, half + 1)

    def to_x(src, dst, send, recv):
        return pltpu.make_async_remote_copy(
            src_ref=src, dst_ref=dst, send_sem=send, recv_sem=recv,
            device_id={"layer": other, "band": b}, device_id_type=MESH)

    def to_band(src, dst, send, recv, peer):
        return pltpu.make_async_remote_copy(
            src_ref=src, dst_ref=dst, send_sem=send, recv_sem=recv,
            device_id={"layer": layer, "band": peer}, device_id_type=MESH)

    h_across = [
        to_x(h_hbm.at[b, pl.ds(0, 5)], hx.at[b, pl.ds(0, 5)], hx_send.at[0], hx_recv.at[0]),
        to_x(h_hbm.at[b, pl.ds(own_cross, 1)], hx.at[b, pl.ds(5, 1)], hx_send.at[1], hx_recv.at[1]),
    ]
    n_across = to_x(nbr_hbm, nx_v, n_send.at[0], n_recv.at[0])
    c_across = [
        to_x(c_hbm.at[:, :, pl.ds(lo, n)], cx[i], c_send.at[i], c_recv.at[i])
        for i, (lo, n) in enumerate(spans)
    ]
    for copy in h_across + [n_across] + c_across:
        copy.start()
    for i, (lo, n) in enumerate(spans):
        copy = pltpu.make_async_copy(c_hbm.at[:, :, pl.ds(lo, n)], cown[i], lc_sem.at[i])
        copy.start()
        c_copies.append(copy)
    for copy in h_copies:
        copy.start()

    sent = []

    def forward(block, peer):
        slot = len(sent)
        copy = to_band(hx.at[block], hx.at[block], f_send.at[slot], f_recv.at[block], peer)
        copy.start()
        sent.append(copy)

    def arrived(block, peer):
        to_band(hx.at[block], hx.at[block], f_send.at[0], f_recv.at[block], peer).wait_recv()

    y_peer = ident(z, 1 - y, core)
    for copy in h_across:
        copy.wait_recv()
    for k in range(1, nz):
        forward(b, ident((z + k) % nz, y, core))
    forward(b, y_peer)
    forward(b, core_peer)
    for k in range(1, nz):
        block = ident((z - k + nz) % nz, y, core)
        arrived(block, block)
        forward(block, y_peer)
        forward(block, core_peer)
    for k in range(nz):
        block = ident((z - k + nz) % nz, 1 - y, core)
        arrived(block, y_peer)
        forward(block, core_peer)
    for k in range(nz):
        for yy in (y, 1 - y):
            arrived(ident((z - k + nz) % nz, yy, 1 - core), core_peer)

    n_across.wait_recv()
    nx_copy = pltpu.make_async_copy(nx_v, nx, misc_sem.at[1])
    nx_copy.start()
    n_copy.wait()
    nx_copy.wait()
    for copy in h_copies:
        copy.wait()

    def image(blocks, table, e, cross, near, far):
        row = jnp.concatenate([blocks[e, k] for k in range(6)], axis=1)
        parts = [near[lax.rem(table[k, e], elements)] for k in range(5)]
        parts.append(far[lax.rem(table[cross, e], elements)])
        return jnp.dot(row, jnp.concatenate(parts, axis=0), preferred_element_type=jnp.float32)

    out_copies = []
    for i, (lo, n) in enumerate(spans):
        c_copies[i].wait()
        c_across[i].wait_recv()

        last = i == count - 1
        start = pl.multiple_of(b * nbl + lo, 128)
        weight = (1 + occ_ref[:, pl.ds(start, n)]).astype(jnp.float32)

        def first_own(e):
            got = image(hown, nown, e, own_cross, cown[i], cx[i])
            return ((got - center * cown[i][e].astype(jnp.float32)) * (1.0 / half_width)).astype(jnp.bfloat16)

        def first_x(e):
            got = image(hx, nx, e, x_cross, cx[i], cown[i])
            return ((got - center * cx[i][e].astype(jnp.float32)) * (1.0 / half_width)).astype(jnp.bfloat16)

        step = 2 if last and elements % 2 == 0 else 1

        def first(t, carry):
            at = [t * step + u for u in range(step)]
            mine = [first_own(e) for e in at]
            theirs = [first_x(e) for e in at]
            for e, a, c in zip(at, mine, theirs):
                f1o[i][e] = a
                f1x[i][e] = c
            return carry

        def second(e):
            got = image(hown, nown, e, own_cross, f1o[i], f1x[i])
            once = f1o[i][e].astype(jnp.float32)
            value = (got - center * once) * (2.0 / half_width) - cown[i][e].astype(jnp.float32)
            value = value.astype(jnp.bfloat16)
            scaled = (value.astype(jnp.float32) * weight).astype(jnp.bfloat16)
            part = lax.dot_general(scaled, value, (((1,), (1,)), ((), ())), preferred_element_type=jnp.float32)
            return value, part + gram[e] if i > 0 else part

        def second_plain(s, carry):
            at = [2 * s, 2 * s + 1]
            got = [second(e) for e in at]
            for e, (value, part) in zip(at, got):
                outv[i][e] = value
                gram[e] = part
            return carry

        def to_core(t):
            return to_band(gsend.at[2 * t + 1 - core], gcore.at[t], k_send.at[t], k_recv.at[t], core_peer)

        def to_owner(k):
            element = (site + k) % half * 2 + core
            return to_band(gsend.at[element], grecv.at[k], g_send.at[k], g_recv.at[k], element)

        def pair_up(s, carry):
            at = [2 * s, 2 * s + 1]
            got = [second(2 * t + 1 - core) for t in at]
            for t, (value, part) in zip(at, got):
                outv[i][2 * t + 1 - core] = value
                gsend[2 * t + 1 - core] = part.astype(jnp.bfloat16)
                to_core(t).start()
            return carry

        def hand_over(ks):
            places = [(site + k) % half for k in ks]
            got = [second(2 * t + core) for t in places]
            for k, t, (value, part) in zip(ks, places, got):
                outv[i][2 * t + core] = value
                to_core(t).wait_recv()
                part = part + gcore[t].astype(jnp.float32)
                if isinstance(k, int) and k == half:
                    gram[2 * t + core] = part
                else:
                    gsend[2 * t + core] = part.astype(jnp.bfloat16)
                    to_owner(k).start()

        def hand_over_two(s, carry):
            hand_over([2 * s + 1, 2 * s + 2])
            return carry

        lax.fori_loop(0, elements // step, first, 0)
        if last:
            lax.fori_loop(0, half // 2, pair_up, 0)
            lax.fori_loop(0, half // 2 - 1, hand_over_two, 0)
            hand_over([half - 1, half])
        else:
            lax.fori_loop(0, elements // 2, second_plain, 0)
        copy = pltpu.make_async_copy(outv[i], filt_hbm.at[:, :, pl.ds(lo, n)], lo_sem.at[i])
        copy.start()
        out_copies.append(copy)

    total = gram[b]
    for k in range(1, half):
        to_owner(k).wait_recv()
        total = total + grecv[k].astype(jnp.float32)
    total_ref[...] = total * (1.0 / (2.0 * nbl * nb))

    for copy in h_across + [n_across] + c_across + sent:
        copy.wait_send()
    for t in range(half):
        to_core(t).wait_send()
    for k in range(1, half):
        to_owner(k).wait_send()
    for copy in out_copies:
        copy.wait()


def finish_kernel(pieces, filt_hbm, total_ref, basis_ref, out_hbm, dens_ref, held, in_sem, out_sem):
    size = held.shape[0] // pieces
    spans = [pl.ds(i * size, size) for i in range(pieces)]
    loads = [pltpu.make_async_copy(filt_hbm.at[at], held.at[at], in_sem.at[i]) for i, at in enumerate(spans)]
    stores = [pltpu.make_async_copy(held.at[at], out_hbm.at[at], out_sem.at[i]) for i, at in enumerate(spans)]
    for load in loads:
        load.start()
    for load, store in zip(loads, stores):
        load.wait()
        store.start()
    total = total_ref[...]
    high = total.astype(jnp.bfloat16)
    low = (total - high.astype(jnp.float32)).astype(jnp.bfloat16)
    functions = basis_ref[0]
    image_g = jnp.dot(functions, high, preferred_element_type=jnp.float32)
    image_g = image_g + jnp.dot(functions, low, preferred_element_type=jnp.float32)
    product = image_g * functions.astype(jnp.float32)
    top = product.astype(jnp.bfloat16)
    rest = (product - top.astype(jnp.float32)).astype(jnp.bfloat16)
    ones = jnp.ones((16, product.shape[1]), jnp.bfloat16)
    over_last = (((1,), (1,)), ((), ()))
    density = lax.dot_general(ones, top, over_last, preferred_element_type=jnp.float32)
    density = density + lax.dot_general(ones, rest, over_last, preferred_element_type=jnp.float32)
    dens_ref[...] = density[0:1]
    for store in stores:
        store.wait()


def plane_body(nb, coeffs, hamilton, neighbors, basis, occupation):
    elements, nbasis, nbl = coeffs.shape
    points = basis.shape[1]
    spans, lo = [], 0
    while lo < nbl:
        n = min(256, nbl - lo)
        spans.append((lo, n))
        lo += n
    count = len(spans)
    width = neighbors.shape[1]
    pieces = 4 if elements % 4 == 0 else 1
    values = [pltpu.VMEM((elements, nbasis, n), jnp.bfloat16) for _, n in spans]
    dma = pltpu.SemaphoreType.DMA
    hbm = pl.BlockSpec(memory_space=pl.ANY)
    vmem = pl.BlockSpec(memory_space=pltpu.VMEM)
    forwards = (nb // 4 - 1) + 2 + 2 * (nb // 4 - 1) + nb // 4
    spread, total = pl.pallas_call(
        functools.partial(kernel, spans, nb),
        out_shape=(
            jax.ShapeDtypeStruct(coeffs.shape, jnp.bfloat16),
            jax.ShapeDtypeStruct((nbasis, nbasis), jnp.float32),
        ),
        in_specs=[hbm, hbm, hbm, vmem],
        out_specs=(hbm, vmem),
        scratch_shapes=values * 5 + [
            pltpu.VMEM((elements, 6, nbasis, nbasis), jnp.bfloat16),
            pltpu.VMEM((elements, 6, nbasis, nbasis), jnp.bfloat16),
            pltpu.VMEM((width, elements), jnp.int32),
            pltpu.SMEM((width, elements), jnp.int32),
            pltpu.SMEM((width, elements), jnp.int32),
            pltpu.VMEM((elements, nbasis, nbasis), jnp.float32),
            pltpu.VMEM((elements, nbasis, nbasis), jnp.bfloat16),
            pltpu.VMEM((nb // 2, nbasis, nbasis), jnp.bfloat16),
            pltpu.VMEM((nb // 2, nbasis, nbasis), jnp.bfloat16),
            dma((count,)), dma((count,)),
            dma((2,)), dma((2,)),
            dma((1,)), dma((1,)),
            dma((forwards,)), dma((nb,)),
            dma((nb // 2,)), dma((nb // 2,)),
            dma((nb // 2,)), dma((nb // 2,)),
            dma((count,)), dma((2,)), dma((count,)), dma((2,)),
        ],
        compiler_params=pltpu.CompilerParams(collective_id=0, has_side_effects=True),
    )(coeffs, hamilton, neighbors.T, occupation.reshape(1, -1))
    return pl.pallas_call(
        functools.partial(finish_kernel, pieces),
        out_shape=(
            jax.ShapeDtypeStruct(coeffs.shape, jnp.bfloat16),
            jax.ShapeDtypeStruct((1, points), jnp.float32),
        ),
        in_specs=[hbm, vmem, vmem],
        out_specs=(hbm, vmem),
        scratch_shapes=[pltpu.VMEM(coeffs.shape, jnp.bfloat16), dma((pieces,)), dma((pieces,))],
    )(spread, total, basis)


def solution(mesh):
    layers, nb = mesh.shape["layer"], mesh.shape["band"]

    def body(coeffs, hamilton, neighbors, basis, occupation):
        elements = coeffs.shape[0]
        one_kernel = (
            layers == 2 and elements == FY * FZ and nb == elements
            and nb % 4 == 0 and nb >= 8 and coeffs.shape[2] % 128 == 0 and basis.shape[0] == 1
        )
        if one_kernel:
            return plane_body(nb, coeffs, hamilton, neighbors, basis, occupation)
        return general_body(coeffs, hamilton, neighbors, basis, occupation)

    return jax.shard_map(
        body,
        mesh=mesh,
        in_specs=(
            P("layer", None, "band"),
            P("layer", None, None, None),
            P("layer", None),
            P(("layer", "band"), None, None),
            P(),
        ),
        out_specs=(P("layer", None, "band"), P(("layer", "band"), None)),
        check_vma=False,
    )
```
